256 devices in a mesh: group: 16 (over x_hi, z), dev: 16 (over x_lo, y, core).
Axes of the slice: x: 4 (x_hi: 2, x_lo: 2; x = x_hi * 2 + x_lo), y: 4, z: 8, core: 2. Of those that a mesh axis runs over, the one named last changes fastest.
Arguments:
- expert_input: bfloat16 [2, 1536, 4096], P(None, ('group', 'dev')), may hold values from -6 to 6
- expert_ids: int32 [2, 1536, 2], P(None, ('group', 'dev')), may hold values from 0 to 7, all different within a row; in each aligned block of 6 rows (0 to 5, 6 to 11, ..., all dimensions but the last counted through in order) at most 2 rows name the same one
- combine: float32 [2, 1536, 2], P(None, ('group', 'dev')), may hold values from 0.25 to 1
- gate_weight: bfloat16 [16, 4096, 6144], P('dev', None, 'group'), may hold values from -0.09375 to 0.09375
- up_weight: bfloat16 [16, 4096, 6144], P('dev', None, 'group'), may hold values from -0.09375 to 0.09375
- down_weight: bfloat16 [16, 6144, 4096], P('dev', 'group'), may hold values from -0.0546875 to 0.0546875
Outputs:
- moe_out: bfloat16 [2, 1536, 4096], P(None, ('group', 'dev'))
The draws below stay inside these ranges and needn't reach their ends.
Inputs may be any that keep to these rules, and one draw needn't show every extreme that they name: `expert_ids`: the two experts of a row differ; among the rows of one device in one step no expert is named more than 2 times.
All inputs are finite; a program needn't handle non-finite values.
Results may differ from the reference program's by a relative error of at most 0.017.
Values may be sent and summed in bfloat16 or wider, within the bound.
A program may use at most 64 MiB of HBM per device.

```python
import math
import jax
import jax.numpy as jnp
import numpy as np
from jax import lax

D = 4096
FF = 12288
STEPS = 2
ROWS_DEV = 6
EXPERTS = 8
SLOT = 2
FF_DEV = 384
ROWS = 1536
N_GROUP = 16
N_DEV = 16


def shard_levels(rng, extent, split, least, top_value):
    def one(dim, shards_of):
        heights = jax.random.uniform(jax.random.fold_in(jax.random.fold_in(rng, 6), dim), (shards_of,), jnp.float32, least / len(split), top_value / len(split))
        return jnp.repeat(jnp.exp(heights), extent[dim] // shards_of).reshape((-1,) + (1,) * (len(extent) - dim - 1))

    loudness = one(*split[0])
    for cut in split[1:]:
        loudness = loudness * one(*cut)
    return loudness


def assign_block(key, own, number, rows, amount, top, reach, lean):
    ranking = jax.random.permutation(key, amount)
    heavy_load, ordinary = portions_of(amount, rows * top, reach, lean, True), portions_of(amount, rows * top, reach, lean, False)
    places = jnp.arange(amount)

    def named(lengths, turn):
        used = int((lengths > 0).sum())
        fixed = max(1, used // 4)
        shifted = fixed + (places - fixed + turn * (used - fixed)) % max(1, amount - fixed)
        return jnp.zeros((amount,), jnp.int32).at[ranking[jnp.where(places < fixed, places, shifted)]].set(jnp.asarray(lengths, jnp.int32))

    lengths = jnp.where(number % 4 == 0, named(heavy_load, number // 4), named(ordinary, number - number // 4 - 1))
    mixed = jax.random.permutation(jax.random.fold_in(own, 3), amount)
    source_of, receiver = mixed[0:amount // 2 * 2:2], mixed[1:amount // 2 * 2:2]
    margin = jnp.minimum(lengths[source_of] - 1, reach - lengths[receiver]) // 2
    margin = jnp.where((source_of == ranking[0]) | (receiver == ranking[0]) | (lengths[receiver] == 0), 0, jnp.maximum(margin, 0))
    shifted = jax.random.randint(jax.random.fold_in(own, 4), (amount // 2,), 0, 1 << 20) % (margin + 1)
    lengths = lengths.at[source_of].add(-shifted).at[receiver].add(shifted)
    members = jnp.searchsorted(jnp.cumsum(lengths), jnp.arange(rows * top), side="right").astype(jnp.int32)
    grid = members.reshape(top, rows).T
    grid = grid[jax.random.permutation(jax.random.fold_in(own, 1), rows)]
    turn = jax.random.randint(jax.random.fold_in(own, 2), (rows, 1), 0, top)
    return jnp.take_along_axis(grid, (jnp.arange(top)[None, :] + turn) % top, axis=1)


def portions_of(number_of, total, reach, skew, full):
    portions = [(1 << 20) // math.isqrt(grade ** skew) + 1 for grade in range(1, number_of + 1)]
    largest = reach if full else min(reach, max(-(-total // number_of), total * portions[0] // sum(portions)))
    least = 1 if total - largest >= number_of - 1 else 0
    given, surplus = [largest] + [least] * (number_of - 1), total - largest - least * (number_of - 1)
    while surplus > 0:
        candidates = [i for i in range(1, number_of) if given[i] < largest] or [i for i in range(1, number_of) if given[i] < reach]
        whole, budget = sum([portions[i] for i in candidates]), surplus
        for i in candidates:
            extra = min(reach - given[i], max(1, budget * portions[i] // whole), surplus)
            given[i] = given[i] + extra
            surplus = surplus - extra
    return np.array(given)


def gaussian(stream_key, extent, scale, most, pieces=(), held_as=jnp.bfloat16):
    level = shard_levels(stream_key, extent, pieces, -0.22, 0.18) if pieces else 1.0
    array = jax.random.normal(stream_key, extent, jnp.float32) * scale * level
    return jnp.minimum(jnp.maximum(array, -most), most).astype(held_as)


def setup_inputs(seed: int = 0) -> dict:
    splits = jax.random.split(jax.random.key(seed), 7)
    expert_input = gaussian(splits[0], (STEPS, ROWS, D), 1.0, 6.0, ((1, 256),))
    expert_ids_keys = jax.random.split(jax.random.fold_in(splits[1], 1), STEPS * ROWS // ROWS_DEV)
    expert_ids_turns = jax.random.permutation(jax.random.fold_in(splits[1], 3), STEPS * ROWS // ROWS_DEV)
    expert_ids = jax.vmap(lambda own, number: assign_block(jax.random.fold_in(splits[1], 2), own, number, ROWS_DEV, EXPERTS, 2, SLOT, 2))(expert_ids_keys, expert_ids_turns).reshape((STEPS, ROWS, 2))
    combine = jnp.clip(0.25 + 0.75 * jax.random.uniform(splits[2], (STEPS, ROWS, 2), jnp.float32) ** shard_levels(splits[2], (STEPS, ROWS, 2), ((1, 256),), -0.2, 0.2), 0.25, 1.0)
    gate_weight = gaussian(splits[3], (2 * EXPERTS, D, FF // 2), D ** -0.5, 0.09375, ((0, 16), (2, 16)))
    up_weight = gaussian(splits[4], (2 * EXPERTS, D, FF // 2), D ** -0.5, 0.09375, ((0, 16), (2, 16)))
    down_weight = gaussian(splits[5], (2 * EXPERTS, FF // 2, D), FF ** -0.5, 0.0546875, ((0, 16), (1, 16)))
    return dict(expert_input=expert_input, expert_ids=expert_ids, combine=combine, gate_weight=gate_weight, up_weight=up_weight, down_weight=down_weight)


def reference(expert_input, expert_ids, combine, gate_weight, up_weight, down_weight):
    device_total = N_GROUP * N_DEV
    slot_total = device_total * SLOT
    outputs = []
    for moment in range(STEPS):
        chosen_ids = expert_ids[moment].reshape(device_total, 2 * ROWS_DEV)
        named_hits = (chosen_ids[:, :, None] == jnp.arange(EXPERTS, dtype=jnp.int32)[None, None, :]).astype(jnp.int32)
        earlier = jnp.cumsum(named_hits, 1) - named_hits
        position = jnp.sum(earlier * named_hits, 2)
        buffer_index = (jnp.arange(device_total, dtype=jnp.int32)[:, None] * SLOT + position).astype(jnp.int32)
        row_index = jnp.arange(device_total, dtype=jnp.int32)[:, None] * ROWS_DEV + jnp.arange(2 * ROWS_DEV, dtype=jnp.int32)[None, :] // 2
        table = jnp.zeros((EXPERTS, slot_total), jnp.int32).at[chosen_ids.reshape(-1), buffer_index.reshape(-1)].set(row_index.reshape(-1).astype(jnp.int32))
        filled = jnp.zeros((EXPERTS, slot_total), jnp.float32).at[chosen_ids.reshape(-1), buffer_index.reshape(-1)].set(1.0)
        tokens = expert_input[moment]

        def one_expert(expert):
            picked_rows = jnp.take(tokens, table[expert], axis=0) * filled[expert][:, None].astype(jnp.bfloat16)
            value = jnp.zeros((slot_total, D), jnp.float32)
            for half_index in range(2):
                entry = 2 * expert + half_index
                gate_half = lax.dynamic_index_in_dim(gate_weight, entry, 0, keepdims=False)
                up_half = lax.dynamic_index_in_dim(up_weight, entry, 0, keepdims=False)
                down_half = lax.dynamic_index_in_dim(down_weight, entry, 0, keepdims=False)
                gate_val = jnp.dot(picked_rows, gate_half, preferred_element_type=jnp.float32)
                up_val = jnp.dot(picked_rows, up_half, preferred_element_type=jnp.float32)
                hidden = (jax.nn.silu(gate_val) * up_val).astype(jnp.bfloat16)
                blocks = hidden.reshape(slot_total, N_GROUP, FF_DEV).astype(jnp.float32)
                down_blocks = down_half.reshape(N_GROUP, FF_DEV, D).astype(jnp.float32)
                product = jnp.einsum("sgf,gfx->gsx", blocks, down_blocks).astype(jnp.bfloat16)
                half_sum = jnp.sum(product.astype(jnp.float32), 0).astype(jnp.bfloat16)
                value = value + half_sum.astype(jnp.float32)
            return value

        values = lax.map(one_expert, jnp.arange(EXPERTS, dtype=jnp.int32))
        picked = values[expert_ids[moment], buffer_index.reshape(ROWS, 2)]
        outputs.append(jnp.sum(combine[moment][:, :, None] * picked, 1).astype(jnp.bfloat16))
    return jnp.stack(outputs, 0)
```

```python
import jax
import jax.numpy as jnp
from jax import lax
from jax.experimental import pallas as pl
from jax.experimental.pallas import tpu as pltpu
from jax.sharding import PartitionSpec as P

MESH = pl.DeviceIdType.MESH
NX, NY, NZ = 4, 4, 8
D, FFD = 4096, 384
BLK = 64
NC = 4
CW = D // NC
HDR = 128
POS = {0: 0, 1: 1, 7: 2, 2: 3, 6: 4, 3: 5, 5: 6, 4: 7}
GROUPS = ((0, 3), (3, 2), (5, 2), (7, 1))


def kernel(
    msg, wmat, perm, gate, up, down, out,
    raw, hdr_t, sel, xs, wg, wu, wd, h, p, sp, rp, fin, yb, pb, xb,
    own_sem, w_own, w_send, w_recv, x_send, x_recv, y_send, y_recv, y_own,
    g_send, g_recv, r_send, r_recv, b_send, b_recv, b_own, f_send, f_recv, f_own,
):
    g, d = lax.axis_index("group"), lax.axis_index("dev")
    z, x_hi = lax.rem(g, NZ), g // NZ
    core, y, x_lo = lax.rem(d, 2), lax.rem(d // 2, NY), d // (2 * NY)
    x = x_hi * 2 + x_lo

    def dev(xx, yy, zz, cc):
        return ((xx // 2) * NZ + zz, (lax.rem(xx, 2) * NY + yy) * 2 + cc)

    def x_at(j):
        return dev(lax.rem(x + j, NX), y, z, core)

    def y_at(j):
        return dev(x, lax.rem(y + j, NY), z, core)

    def z_at(j):
        return dev(x, y, lax.rem(z + j, NZ), core)

    other = dev(x, y, z, 1 - core)

    def remote(src, dst, send, recv, to):
        return pltpu.make_async_remote_copy(
            src_ref=src, dst_ref=dst, send_sem=send, recv_sem=recv, device_id=to, device_id_type=MESH
        )

    def cols(c):
        return pl.ds(c * CW, CW)

    def rows16(i):
        return pl.ds(pl.multiple_of(i * 16, 16), 16)

    sends = []

    def start(copy):
        copy.start()
        sends.append(copy)

    own = pltpu.make_async_copy(msg, raw.at[pl.ds(0, 16), :], own_sem)
    own.start()
    w_copies = [
        pltpu.make_async_copy(gate, wg.at[:, pl.ds(0, FFD)], w_own.at[0]),
        pltpu.make_async_copy(up, wu.at[:, pl.ds(0, FFD)], w_own.at[1]),
        pltpu.make_async_copy(down, wd.at[pl.ds(0, FFD), :], w_own.at[2]),
    ]
    barrier = pltpu.get_barrier_semaphore()
    partners = [x_at(j) for j in (1, 2, 3)] + [y_at(j) for j in (1, 2, 3)] + [z_at(1), z_at(NZ - 1), other]
    for partner in partners:
        pl.semaphore_signal(barrier, inc=1, device_id=partner, device_id_type=MESH)
    pl.semaphore_wait(barrier, len(partners))

    def x_copy(j, c):
        part = pl.ds(D, HDR) if c == NC else cols(c)
        return remote(
            msg.at[:, part], raw.at[pl.ds(j * 16, 16), part], x_send.at[j - 1, c], x_recv.at[j - 1, c], x_at(j)
        )

    x_copies = {}
    for c in (NC, 0, 1, 2, 3):
        for j in (1, 3, 2):
            x_copies[j, c] = x_copy(j, c)
            start(x_copies[j, c])
    for copy in w_copies:
        copy.start()
    w_remote = [
        remote(gate, wg.at[:, pl.ds(FFD, FFD)], w_send.at[0], w_recv.at[0], other),
        remote(up, wu.at[:, pl.ds(FFD, FFD)], w_send.at[1], w_recv.at[1], other),
        remote(down, wd.at[pl.ds(FFD, FFD), :], w_send.at[2], w_recv.at[2], other),
    ]
    for copy in w_remote:
        start(copy)

    y_copies = {}

    def pick(c):
        if c == 0:
            own.wait()
            for j in (1, 2, 3):
                x_copies[j, NC].wait_recv()
            hdr_t[...] = raw[:, pl.ds(D, HDR)].astype(jnp.float32).T.astype(jnp.bfloat16)
        for j in (1, 2, 3):
            x_copies[j, c].wait_recv()
        sel[:, cols(c)] = jnp.dot(
            hdr_t[...], raw[:, cols(c)], preferred_element_type=jnp.float32
        ).astype(jnp.bfloat16)
        for j in (1, 3, 2):
            to = lax.rem(y + j, NY)
            y_copies[j, c] = remote(
                sel.at[rows16(x_lo * 4 + to), cols(c)], xs.at[rows16(y), cols(c)],
                y_send.at[j - 1, c], y_recv.at[j - 1, c], y_at(j),
            )
            start(y_copies[j, c])
        y_copies[0, c] = pltpu.make_async_copy(
            sel.at[rows16(x_lo * 4 + y), cols(c)], xs.at[rows16(y), cols(c)], y_own.at[c]
        )
        y_copies[0, c].start()

    def block(k):
        return pl.ds(POS[k] * BLK, BLK)

    def g_copy(way, hop, c):
        k_from, k_to = ((NZ - hop) % NZ, NZ - hop - 1) if way == 0 else (hop, hop + 1)
        return remote(
            xs.at[block(k_from), cols(c)], xs.at[block(k_to), cols(c)],
            g_send.at[way, hop, c], g_recv.at[way, hop, c], z_at(1 if way == 0 else NZ - 1),
        )

    def far(way):
        return (0, 1) if way == 0 else (2, 3)

    g_copies = {}

    def g_start(way, hop, c):
        g_copies[way, hop, c] = g_copy(way, hop, c)
        start(g_copies[way, hop, c])

    order = {0: (0, 1, 2, 3), 1: (2, 3, 0, 1)}

    def z_first(c):
        for j in (1, 2, 3):
            y_copies[j, c].wait_recv()
        y_copies[0, c].wait()
        for way in (0, 1):
            g_start(way, 0, c)

    def z_next(hop, which):
        for i in which:
            for way in (0, 1):
                c = order[way][i]
                if hop == 3 and c not in far(way):
                    continue
                g_copies[way, hop, c].wait_recv()
                if hop < 2 or (hop == 2 and c in far(way)):
                    g_start(way, hop + 1, c)

    pick(0)
    pick(1)
    z_first(0)
    pick(2)
    z_first(1)
    pick(3)
    z_first(2)
    z_first(3)

    def gate_up(group):
        first, count = GROUPS[group]
        rows, live = pl.ds(first * BLK, count * BLK), pl.ds(0, count * BLK)

        def tile(n, carry):
            part = pl.ds(pl.multiple_of(n * 256, 256), 256)
            gate_val = jnp.dot(xs[rows, :], wg[:, part], preferred_element_type=jnp.float32)
            up_val = jnp.dot(xs[rows, :], wu[:, part], preferred_element_type=jnp.float32)
            h[live, part] = (jax.nn.silu(gate_val) * up_val).astype(jnp.bfloat16)
            return carry

        lax.fori_loop(0, 2 * FFD // 256, tile, 0)

    def down_proj(group):
        first, count = GROUPS[group]
        rows, live = pl.ds(first * BLK, count * BLK), pl.ds(0, count * BLK)

        def tile(n, carry):
            part = pl.ds(pl.multiple_of(n * 256, 256), 256)
            p[rows, part] = jnp.dot(h[live, :], wd[:, part], preferred_element_type=jnp.float32)
            return carry

        lax.fori_loop(0, D // 256, tile, 0)

    z_next(0, (0, 1, 2, 3))
    for copy in w_copies:
        copy.wait()
    for copy in w_remote:
        copy.wait_recv()
    gate_up(0)
    z_next(1, (0, 1))
    down_proj(0)
    z_next(1, (2, 3))
    gate_up(1)
    z_next(2, (0, 1))
    down_proj(1)
    z_next(2, (2, 3))
    gate_up(2)
    down_proj(2)

    def held(way, hop):
        return 4 - hop if way == 0 else (4 + hop) % NZ

    r_copies = {}

    def r_start(way, hop, c):
        r_copies[way, hop, c] = remote(
            sp.at[way, hop, :, cols(c)], rp.at[way, hop, :, cols(c)],
            r_send.at[way, hop, c], r_recv.at[way, hop, c], z_at(1 if way == 0 else NZ - 1),
        )
        start(r_copies[way, hop, c])

    def r_own(way, hop, c):
        sp[way, hop, :, cols(c)] = p[block(held(way, hop)), cols(c)].astype(jnp.bfloat16)
        r_start(way, hop, c)

    def r_add(way, hop, c):
        r_copies[way, hop - 1, c].wait_recv()
        sp[way, hop, :, cols(c)] = (
            p[block(held(way, hop)), cols(c)] + rp[way, hop - 1, :, cols(c)].astype(jnp.float32)
        ).astype(jnp.bfloat16)
        r_start(way, hop, c)

    near = {0: (2, 3), 1: (0, 1)}
    for i in (0, 1):
        for way in (0, 1):
            r_own(way, 1, near[way][i])
    z_next(3, (0, 1))
    gate_up(3)
    down_proj(3)
    for i in (0, 1):
        for way in (0, 1):
            r_own(way, 0, far(way)[i])
    for hop in (1, 2, 3):
        for which, step in ((near, hop + 1), ({0: far(0), 1: far(1)}, hop)):
            if step > 3:
                continue
            for i in (0, 1):
                for way in (0, 1):
                    r_add(way, step, which[way][i])

    b_copies = {}

    def back_y(c):
        for way in (0, 1):
            r_copies[way, 3, c].wait_recv()
        fin[:, cols(c)] = (
            p[block(0), cols(c)]
            + rp[0, 3, :, cols(c)].astype(jnp.float32)
            + rp[1, 3, :, cols(c)].astype(jnp.float32)
        ).astype(jnp.bfloat16)
        for j in (1, 3, 2):
            to = lax.rem(y + j, NY)
            b_copies[j, c] = remote(
                fin.at[rows16(to), cols(c)], yb.at[rows16(y), cols(c)],
                b_send.at[j - 1, c], b_recv.at[j - 1, c], y_at(j),
            )
            start(b_copies[j, c])
        b_copies[0, c] = pltpu.make_async_copy(
            fin.at[rows16(y), cols(c)], yb.at[rows16(y), cols(c)], b_own.at[c]
        )
        b_copies[0, c].start()

    f_copies = {}

    def back_x(c):
        for j in (1, 2, 3):
            b_copies[j, c].wait_recv()
        b_copies[0, c].wait()
        pb[:, cols(c)] = jnp.dot(perm[...], yb[:, cols(c)], preferred_element_type=jnp.float32).astype(jnp.bfloat16)
        for j in (1, 3, 2):
            to = lax.rem(x + j, NX)
            f_copies[j, c] = remote(
                pb.at[rows16(to), cols(c)], xb.at[rows16(x), cols(c)],
                f_send.at[j - 1, c], f_recv.at[j - 1, c], x_at(j),
            )
            start(f_copies[j, c])
        f_copies[0, c] = pltpu.make_async_copy(
            pb.at[rows16(x), cols(c)], xb.at[rows16(x), cols(c)], f_own.at[c]
        )
        f_copies[0, c].start()

    def finish(c):
        for j in (1, 2, 3):
            f_copies[j, c].wait_recv()
        f_copies[0, c].wait()
        out[:, cols(c)] = jnp.dot(
            wmat[...], xb[:, cols(c)].astype(jnp.float32),
            preferred_element_type=jnp.float32, precision=lax.Precision.HIGHEST,
        ).astype(jnp.bfloat16)

    back_y(0)
    back_y(2)
    back_x(0)
    back_y(1)
    back_x(2)
    back_y(3)
    finish(0)
    back_x(1)
    finish(2)
    back_x(3)
    finish(1)
    finish(3)
    for copy in sends:
        copy.wait_send()


def local(expert_input, expert_ids, combine, gate_weight, up_weight, down_weight):
    steps, rows = expert_input.shape[0], expert_input.shape[1]
    x = (lax.axis_index("group") // NZ) * 2 + lax.axis_index("dev") // (2 * NY)
    ids = expert_ids.reshape(steps, 2 * rows)
    order = jnp.arange(2 * rows)
    earlier = (ids[:, :, None] == ids[:, None, :]) & (order[None, :] < order[:, None])[None]
    slot = jnp.sum(earlier.astype(jnp.int32), 2) + 2 * jnp.arange(steps)[:, None]
    pad = ((0, 0), (0, 8 - rows), (0, 0))
    ids = jnp.pad(ids.reshape(steps, rows, 2), pad, constant_values=-1).reshape(16, 2)
    slot = jnp.pad(slot.reshape(steps, rows, 2), pad).reshape(16, 2)
    weight = jnp.pad(combine, pad).reshape(16, 2)
    place = (ids // 4) * 64 + lax.rem(ids, 4) * 16 + x * 4 + slot
    place = jnp.where(ids < 0, -1, place)
    header = jnp.any(place[:, :, None] == jnp.arange(HDR), 1).astype(jnp.bfloat16)
    col = jnp.arange(64)
    expert, col_slot = lax.rem(col // 16, 2) * 4 + lax.rem(col // 4, 4), lax.rem(col, 4)
    hit = (ids[:, :, None] == expert) & (slot[:, :, None] == col_slot)
    wmat = jnp.sum(jnp.where(hit, weight[:, :, None], 0.0), 1)
    perm = (
        ((col // 16)[:, None] == lax.rem(col // 4, 4)[None, :])
        & (lax.rem(col // 4, 4)[:, None] == (col // 16)[None, :])
        & (col_slot[:, None] == col_slot[None, :])
    ).astype(jnp.bfloat16)
    msg = jnp.concatenate([jnp.pad(expert_input, pad).reshape(16, D), header], 1)
    bf, vm = jnp.bfloat16, pltpu.VMEM
    dma = pltpu.SemaphoreType.DMA
    result = pl.pallas_call(
        kernel,
        out_shape=jax.ShapeDtypeStruct((16, D), bf),
        in_specs=[
            pl.BlockSpec(memory_space=pl.ANY),
            pl.BlockSpec(memory_space=pltpu.VMEM),
            pl.BlockSpec(memory_space=pltpu.VMEM),
            pl.BlockSpec(memory_space=pl.ANY),
            pl.BlockSpec(memory_space=pl.ANY),
            pl.BlockSpec(memory_space=pl.ANY),
        ],
        out_specs=pl.BlockSpec(memory_space=pltpu.VMEM),
        scratch_shapes=[
            vm((64, D + HDR), bf), vm((HDR, 64), bf), vm((HDR, D), bf), vm((NZ * BLK, D), bf),
            vm((D, 2 * FFD), bf), vm((D, 2 * FFD), bf), vm((2 * FFD, D), bf),
            vm((3 * BLK, 2 * FFD), bf), vm((NZ * BLK, D), jnp.float32),
            vm((2, 4, BLK, D), bf), vm((2, 4, BLK, D), bf),
            vm((BLK, D), bf), vm((64, D), bf), vm((64, D), bf), vm((64, D), bf),
            dma, dma((3,)), dma((3,)), dma((3,)),
            dma((3, NC + 1)), dma((3, NC + 1)), dma((3, NC)), dma((3, NC)), dma((NC,)),
            dma((2, 4, NC)), dma((2, 4, NC)), dma((2, 4, NC)), dma((2, 4, NC)),
            dma((3, NC)), dma((3, NC)), dma((NC,)), dma((3, NC)), dma((3, NC)), dma((NC,)),
        ],
        compiler_params=pltpu.CompilerParams(
            collective_id=0, has_side_effects=True, vmem_limit_bytes=60 * 2**20
        ),
    )(msg, wmat, perm, gate_weight[0], up_weight[0], down_weight[0])
    return result.reshape(steps, 8, D)[:, :rows]


def solution(mesh):
    in_specs = (
        P(None, ("group", "dev"), None),
        P(None, ("group", "dev"), None),
        P(None, ("group", "dev"), None),
        P("dev", None, "group"),
        P("dev", None, "group"),
        P("dev", "group", None),
    )
    out_specs = P(None, ("group", "dev"), None)
    return jax.shard_map(local, mesh=mesh, in_specs=in_specs, out_specs=out_specs, check_vma=False)
```

```python
import jax
import jax.numpy as jnp
from jax import lax
from jax.experimental import pallas as pl
from jax.experimental.pallas import tpu as pltpu
from jax.sharding import PartitionSpec as P

MESH = pl.DeviceIdType.MESH
NX, NY, NZ = 4, 4, 8
D, FFD = 4096, 384
BLK = 64
NC = 4
CW = 512
PW = NC * CW
RW = D - PW
HDR = 128
XW = HDR + RW
MW = XW + HDR
POS = {0: 0, 1: 1, 7: 2, 2: 3, 6: 4, 3: 5, 5: 6, 4: 7}
GROUPS = ((0, 3), (3, 2), (5, 2), (7, 1))


def kernel(
    msg, wmat, gate, up, down, out,
    raw, hdr_t, sel, xs, wg, wu, wd, h, p, sp, rp, fin, yb, pb, xb,
    perm, xr, selr, finr, ybr, pbr, xbr, pr, spr, rpr,
    own_sem, w_own, w_send, w_recv, x_send, x_recv, y_send, y_recv, y_own,
    g_send, g_recv, r_send, r_recv, b_send, b_recv, b_own, f_send, f_recv, f_own,
    rz_send, rz_recv, rx_send, rx_recv, ry_send, ry_recv, ry_own,
    rb_send, rb_recv, rb_own, rf_send, rf_recv, rf_own, rr_send, rr_recv,
):
    g, d = lax.axis_index("group"), lax.axis_index("dev")
    z, x_hi = lax.rem(g, NZ), g // NZ
    core, y, x_lo = lax.rem(d, 2), lax.rem(d // 2, NY), d // (2 * NY)
    x = x_hi * 2 + x_lo

    def dev(xx, yy, zz, cc):
        return ((xx // 2) * NZ + zz, (lax.rem(xx, 2) * NY + yy) * 2 + cc)

    def x_at(j):
        return dev(lax.rem(x + j, NX), y, z, core)

    def y_at(j):
        return dev(x, lax.rem(y + j, NY), z, core)

    def z_at(j):
        return dev(x, y, lax.rem(z + j, NZ), core)

    other = dev(x, y, z, 1 - core)

    def remote(src, dst, send, recv, to):
        return pltpu.make_async_remote_copy(
            src_ref=src, dst_ref=dst, send_sem=send, recv_sem=recv, device_id=to, device_id_type=MESH
        )

    def cols(c):
        return pl.ds(c * CW, CW)

    def rows16(i):
        return pl.ds(pl.multiple_of(i * 16, 16), 16)

    sends = []

    def start(copy):
        copy.start()
        sends.append(copy)

    own = pltpu.make_async_copy(msg.at[:, pl.ds(0, PW + HDR)], raw.at[pl.ds(0, 16), :], own_sem.at[0])
    own.start()
    own_r = pltpu.make_async_copy(msg.at[:, pl.ds(PW, MW)], xr.at[0, pl.ds(0, 16), :], own_sem.at[1])
    own_r.start()
    w_copies = [
        pltpu.make_async_copy(gate, wg.at[:, pl.ds(0, FFD)], w_own.at[0]),
        pltpu.make_async_copy(up, wu.at[:, pl.ds(0, FFD)], w_own.at[1]),
        pltpu.make_async_copy(down, wd.at[pl.ds(0, FFD), :], w_own.at[2]),
    ]
    barrier = pltpu.get_barrier_semaphore()
    partners = [x_at(j) for j in (1, 2, 3)] + [y_at(j) for j in (1, 2, 3)] + [z_at(1), z_at(NZ - 1), other]
    for partner in partners:
        pl.semaphore_signal(barrier, inc=1, device_id=partner, device_id_type=MESH)
    pl.semaphore_wait(barrier, len(partners))

    a, b = lax.broadcasted_iota(jnp.int32, (64, 64), 0), lax.broadcasted_iota(jnp.int32, (64, 64), 1)
    moved = (b & 3) | ((b >> 4) << 2) | (((b >> 2) & 3) << 4)
    perm[...] = jnp.where(a == moved, 1.0, 0.0).astype(jnp.bfloat16)

    rz_copies = {}

    def rz_start(way, hop):
        k_from, k_to = ((NZ - hop) % NZ, NZ - hop - 1) if way == 0 else (hop, hop + 1)
        part = pl.ds(0, MW) if hop < 3 else pl.ds(way * (MW // 2), MW // 2)
        rows = pl.ds(0, 16)
        source = msg.at[:, pl.ds(PW, MW)] if hop == 0 else xr.at[k_from, rows, part]
        rz_copies[way, hop] = remote(
            source, xr.at[k_to, rows, part], rz_send.at[way, hop], rz_recv.at[way, hop], z_at(1 if way == 0 else NZ - 1)
        )
        start(rz_copies[way, hop])

    rx_copies, ry_copies = {}, {}

    def rx_start(k):
        for j in (1, 3, 2):
            part = pl.ds(0, XW)
            source = msg.at[:, pl.ds(PW, XW)] if k == 0 else xr.at[k, pl.ds(0, 16), part]
            rx_copies[k, j] = remote(
                source, xr.at[k, pl.ds(j * 16, 16), part], rx_send.at[k, j - 1], rx_recv.at[k, j - 1], x_at(j)
            )
            start(rx_copies[k, j])

    def rz_next(hop):
        if hop == 3:
            for way in (0, 1):
                rz_copies[way, 3].wait_recv()
            rx_start(4)
            return
        for way in (0, 1):
            rz_copies[way, hop].wait_recv()
            rz_start(way, hop + 1)
        for way in (0, 1):
            rx_start(NZ - hop - 1 if way == 0 else hop + 1)

    def r_pick(k):
        if k == 0:
            own_r.wait()
        for j in (1, 2, 3):
            rx_copies[k, j].wait_recv()
        hdr_t[...] = xr[k, :, pl.ds(0, HDR)].astype(jnp.float32).T.astype(jnp.bfloat16)
        selr[k] = jnp.dot(
            hdr_t[pl.ds(pl.multiple_of(x_lo * 64, 64), 64), :], xr[k, :, pl.ds(HDR, RW)],
            preferred_element_type=jnp.float32,
        ).astype(jnp.bfloat16)
        target = xs.at[pl.ds(pl.multiple_of(POS[k] * BLK + y * 16, 16), 16), pl.ds(PW, RW)]
        for j in (1, 3, 2):
            ry_copies[k, j] = remote(
                selr.at[k, rows16(lax.rem(y + j, NY)), :], target, ry_send.at[k, j - 1], ry_recv.at[k, j - 1], y_at(j)
            )
            start(ry_copies[k, j])
        ry_copies[k, 0] = pltpu.make_async_copy(selr.at[k, rows16(y), :], target, ry_own.at[k])
        ry_copies[k, 0].start()

    def r_ready(k):
        for j in (1, 2, 3):
            ry_copies[k, j].wait_recv()
        ry_copies[k, 0].wait()

    for way in (0, 1):
        rz_start(way, 0)

    def x_copy(j, c):
        part = pl.ds(PW, HDR) if c == NC else cols(c)
        return remote(
            msg.at[:, part], raw.at[pl.ds(j * 16, 16), part], x_send.at[j - 1, c], x_recv.at[j - 1, c], x_at(j)
        )

    x_copies = {}
    for c in (NC, 0, 1, 2, 3):
        for j in (1, 3, 2):
            x_copies[j, c] = x_copy(j, c)
            start(x_copies[j, c])
    rx_start(0)
    for copy in w_copies:
        copy.start()
    w_remote = [
        remote(gate, wg.at[:, pl.ds(FFD, FFD)], w_send.at[0], w_recv.at[0], other),
        remote(up, wu.at[:, pl.ds(FFD, FFD)], w_send.at[1], w_recv.at[1], other),
        remote(down, wd.at[pl.ds(FFD, FFD), :], w_send.at[2], w_recv.at[2], other),
    ]
    for copy in w_remote:
        start(copy)

    y_copies = {}

    def pick(c):
        if c == 0:
            own.wait()
            for j in (1, 2, 3):
                x_copies[j, NC].wait_recv()
        for j in (1, 2, 3):
            x_copies[j, c].wait_recv()
        hdr_t[...] = raw[:, pl.ds(PW, HDR)].astype(jnp.float32).T.astype(jnp.bfloat16)
        sel[:, cols(c)] = jnp.dot(
            hdr_t[pl.ds(pl.multiple_of(x_lo * 64, 64), 64), :], raw[:, cols(c)], preferred_element_type=jnp.float32
        ).astype(jnp.bfloat16)
        for j in (1, 3, 2):
            to = lax.rem(y + j, NY)
            y_copies[j, c] = remote(
                sel.at[rows16(to), cols(c)], xs.at[rows16(y), cols(c)],
                y_send.at[j - 1, c], y_recv.at[j - 1, c], y_at(j),
            )
            start(y_copies[j, c])
        y_copies[0, c] = pltpu.make_async_copy(
            sel.at[rows16(y), cols(c)], xs.at[rows16(y), cols(c)], y_own.at[c]
        )
        y_copies[0, c].start()

    def block(k):
        return pl.ds(POS[k] * BLK, BLK)

    def g_copy(way, hop, c):
        k_from, k_to = ((NZ - hop) % NZ, NZ - hop - 1) if way == 0 else (hop, hop + 1)
        return remote(
            xs.at[block(k_from), cols(c)], xs.at[block(k_to), cols(c)],
            g_send.at[way, hop, c], g_recv.at[way, hop, c], z_at(1 if way == 0 else NZ - 1),
        )

    def far(way):
        return (0, 1) if way == 0 else (2, 3)

    g_copies = {}

    def g_start(way, hop, c):
        g_copies[way, hop, c] = g_copy(way, hop, c)
        start(g_copies[way, hop, c])

    order = {0: (0, 1, 2, 3), 1: (2, 3, 0, 1)}

    def z_first(c):
        for j in (1, 2, 3):
            y_copies[j, c].wait_recv()
        y_copies[0, c].wait()
        for way in (0, 1):
            g_start(way, 0, c)

    def z_next(hop, which):
        for i in which:
            for way in (0, 1):
                c = order[way][i]
                if hop == 3 and c not in far(way):
                    continue
                g_copies[way, hop, c].wait_recv()
                if hop < 2 or (hop == 2 and c in far(way)):
                    g_start(way, hop + 1, c)

    pick(0)
    rz_next(0)
    pick(1)
    z_first(0)
    rz_next(1)
    pick(2)
    z_first(1)
    pick(3)
    rz_next(2)
    z_first(2)
    z_first(3)
    rz_next(3)

    def gate_up(group, n):
        first, count = GROUPS[group]
        rows, part = pl.ds(first * BLK, count * BLK), pl.ds(n * 256, 256)
        gate_val = jnp.dot(xs[rows, :], wg[:, part], preferred_element_type=jnp.float32)
        up_val = jnp.dot(xs[rows, :], wu[:, part], preferred_element_type=jnp.float32)
        h[rows, part] = (jax.nn.silu(gate_val) * up_val).astype(jnp.bfloat16)

    def down_proj(group, quarter):
        first, count = GROUPS[group]
        rows = pl.ds(first * BLK, count * BLK)

        def tile(n, carry):
            part = pl.ds(pl.multiple_of(n * 256, 256), 256)
            p[rows, part] = jnp.dot(h[rows, :], wd[:, part], preferred_element_type=jnp.float32)
            return carry

        lax.fori_loop(quarter * 4, quarter * 4 + 4, tile, 0)

    def held(way, hop):
        return 4 - hop if way == 0 else (4 + hop) % NZ

    r_copies = {}

    def r_start(way, hop, c):
        r_copies[way, hop, c] = remote(
            sp.at[way, hop, :, cols(c)], rp.at[way, hop, :, cols(c)],
            r_send.at[way, hop, c], r_recv.at[way, hop, c], z_at(1 if way == 0 else NZ - 1),
        )
        start(r_copies[way, hop, c])

    def r_own(way, hop, c):
        sp[way, hop, :, cols(c)] = p[block(held(way, hop)), cols(c)].astype(jnp.bfloat16)
        r_start(way, hop, c)

    def r_add(way, hop, c):
        r_copies[way, hop - 1, c].wait_recv()
        sp[way, hop, :, cols(c)] = (
            p[block(held(way, hop)), cols(c)] + rp[way, hop - 1, :, cols(c)].astype(jnp.float32)
        ).astype(jnp.bfloat16)
        r_start(way, hop, c)

    near = {0: (2, 3), 1: (0, 1)}

    def r_adds(which, step):
        for i in (0, 1):
            for way in (0, 1):
                r_add(way, step, which[way][i])

    rb_copies, rf_copies, rr_copies = {}, {}, {}

    def r_back_y(k):
        finr[k] = p[block(k), pl.ds(PW, RW)].astype(jnp.bfloat16)
        for j in (1, 3, 2):
            rb_copies[k, j] = remote(
                finr.at[k, rows16(lax.rem(y + j, NY)), :], ybr.at[k, rows16(y), :],
                rb_send.at[k, j - 1], rb_recv.at[k, j - 1], y_at(j),
            )
            start(rb_copies[k, j])
        rb_copies[k, 0] = pltpu.make_async_copy(finr.at[k, rows16(y), :], ybr.at[k, rows16(y), :], rb_own.at[k])
        rb_copies[k, 0].start()

    def r_back_x(k):
        for j in (1, 2, 3):
            rb_copies[k, j].wait_recv()
        rb_copies[k, 0].wait()
        pbr[k] = jnp.dot(perm[...], ybr[k], preferred_element_type=jnp.float32).astype(jnp.bfloat16)
        for j in (1, 3, 2):
            rf_copies[k, j] = remote(
                pbr.at[k, rows16(lax.rem(x + j, NX)), :], xbr.at[k, rows16(x), :],
                rf_send.at[k, j - 1], rf_recv.at[k, j - 1], x_at(j),
            )
            start(rf_copies[k, j])
        rf_copies[k, 0] = pltpu.make_async_copy(pbr.at[k, rows16(x), :], xbr.at[k, rows16(x), :], rf_own.at[k])
        rf_copies[k, 0].start()

    def r_weigh(k):
        for j in (1, 2, 3):
            rf_copies[k, j].wait_recv()
        rf_copies[k, 0].wait()
        weights = xr[k, pl.ds(0, 16), pl.ds(XW, HDR)]
        values = xbr[k]
        pr[k] = jnp.dot(weights, jnp.concatenate([values, values], 0), preferred_element_type=jnp.float32)

    def rr_step(way, hop):
        part = pl.ds(0, RW) if hop else pl.ds(way * (RW // 2), RW // 2)
        k = held(way, hop)
        total = pr[k, :, part]
        if hop:
            rr_copies[way, hop - 1].wait_recv()
            if hop == 1:
                half = pl.ds(way * (RW // 2), RW // 2)
                pr[k, :, half] = pr[k, :, half] + rpr[way, 0, :, half].astype(jnp.float32)
                total = pr[k, :, part]
            else:
                total = total + rpr[way, hop - 1, :, part].astype(jnp.float32)
        spr[way, hop, :, part] = total.astype(jnp.bfloat16)
        rr_copies[way, hop] = remote(
            spr.at[way, hop, :, part], rpr.at[way, hop, :, part],
            rr_send.at[way, hop], rr_recv.at[way, hop], z_at(1 if way == 0 else NZ - 1),
        )
        start(rr_copies[way, hop])

    def rr_steps(hop):
        for way in (0, 1):
            rr_step(way, hop)

    def r_finish():
        for way in (0, 1):
            rr_copies[way, 3].wait_recv()
        out[:, pl.ds(PW, RW)] = (
            pr[0] + rpr[0, 3].astype(jnp.float32) + rpr[1, 3].astype(jnp.float32)
        ).astype(jnp.bfloat16)

    r_pick(0)
    z_next(0, (0,))
    r_pick(7)
    z_next(0, (1, 2))
    r_pick(1)
    z_next(0, (3,))
    for copy in w_copies[:2]:
        copy.wait()
    for copy in w_remote[:2]:
        copy.wait_recv()
    for k in (0, 7, 1):
        r_ready(k)
    gate_up(0, 0)
    r_pick(6)
    z_next(1, (0,))
    gate_up(0, 1)
    z_next(1, (1,))
    r_pick(2)
    gate_up(0, 2)
    w_copies[2].wait()
    w_remote[2].wait_recv()
    z_next(1, (2,))
    down_proj(0, 0)
    down_proj(0, 1)
    z_next(1, (3,))
    r_pick(5)
    down_proj(0, 2)
    down_proj(0, 3)
    r_ready(6)
    r_ready(2)
    gate_up(1, 0)
    z_next(2, (0,))
    r_pick(3)
    gate_up(1, 1)
    z_next(2, (1,))
    r_pick(4)
    gate_up(1, 2)
    z_next(2, (2,))
    for k in (0, 7, 1):
        r_back_y(k)
    down_proj(1, 0)
    down_proj(1, 1)
    z_next(2, (3,))
    down_proj(1, 2)
    down_proj(1, 3)
    r_ready(5)
    r_ready(3)
    r_back_y(6)
    r_back_y(2)
    gate_up(2, 0)
    r_back_x(0)
    gate_up(2, 1)
    r_back_x(7)
    gate_up(2, 2)
    r_back_x(1)
    for quarter in range(4):
        down_proj(2, quarter)
    for i in (0, 1):
        for way in (0, 1):
            r_own(way, 1, near[way][i])
    r_back_y(5)
    r_back_y(3)
    z_next(3, (0, 1))
    r_ready(4)
    gate_up(3, 0)
    r_back_x(6)
    gate_up(3, 1)
    r_back_x(2)
    gate_up(3, 2)
    down_proj(3, 0)
    r_own(0, 0, 0)
    down_proj(3, 1)
    r_own(0, 0, 1)
    down_proj(3, 2)
    r_own(1, 0, 2)
    down_proj(3, 3)
    r_own(1, 0, 3)
    r_back_y(4)
    r_back_x(5)
    r_back_x(3)
    r_adds(near, 2)
    for k in (0, 7, 1):
        r_weigh(k)
    r_adds({0: far(0), 1: far(1)}, 1)
    r_back_x(4)
    for k in (6, 2):
        r_weigh(k)
    r_adds(near, 3)
    for k in (5, 3):
        r_weigh(k)
    r_adds({0: far(0), 1: far(1)}, 2)
    r_weigh(4)
    rr_steps(0)
    r_adds({0: far(0), 1: far(1)}, 3)
    rr_steps(1)
    b_copies = {}

    def back_y(c):
        for way in (0, 1):
            r_copies[way, 3, c].wait_recv()
        fin[:, cols(c)] = (
            p[block(0), cols(c)]
            + rp[0, 3, :, cols(c)].astype(jnp.float32)
            + rp[1, 3, :, cols(c)].astype(jnp.float32)
        ).astype(jnp.bfloat16)
        for j in (1, 3, 2):
            to = lax.rem(y + j, NY)
            b_copies[j, c] = remote(
                fin.at[rows16(to), cols(c)], yb.at[rows16(y), cols(c)],
                b_send.at[j - 1, c], b_recv.at[j - 1, c], y_at(j),
            )
            start(b_copies[j, c])
        b_copies[0, c] = pltpu.make_async_copy(
            fin.at[rows16(y), cols(c)], yb.at[rows16(y), cols(c)], b_own.at[c]
        )
        b_copies[0, c].start()

    f_copies = {}

    def back_x(c):
        for j in (1, 2, 3):
            b_copies[j, c].wait_recv()
        b_copies[0, c].wait()
        pb[:, cols(c)] = jnp.dot(perm[...], yb[:, cols(c)], preferred_element_type=jnp.float32).astype(jnp.bfloat16)
        for j in (1, 3, 2):
            to = lax.rem(x + j, NX)
            f_copies[j, c] = remote(
                pb.at[rows16(to), cols(c)], xb.at[rows16(x), cols(c)],
                f_send.at[j - 1, c], f_recv.at[j - 1, c], x_at(j),
            )
            start(f_copies[j, c])
        f_copies[0, c] = pltpu.make_async_copy(
            pb.at[rows16(x), cols(c)], xb.at[rows16(x), cols(c)], f_own.at[c]
        )
        f_copies[0, c].start()

    def finish(c):
        for j in (1, 2, 3):
            f_copies[j, c].wait_recv()
        f_copies[0, c].wait()
        out[:, cols(c)] = jnp.dot(
            wmat[...], xb[:, cols(c)].astype(jnp.float32),
            preferred_element_type=jnp.float32, precision=lax.Precision.HIGHEST,
        ).astype(jnp.bfloat16)

    back_y(0)
    back_y(2)
    rr_steps(2)
    back_x(0)
    back_y(1)
    back_x(2)
    back_y(3)
    rr_steps(3)
    finish(0)
    back_x(1)
    finish(2)
    back_x(3)
    r_finish()
    finish(1)
    finish(3)
    for copy in sends:
        copy.wait_send()


def local(expert_input, expert_ids, combine, gate_weight, up_weight, down_weight):
    steps, rows = expert_input.shape[0], expert_input.shape[1]
    x = (lax.axis_index("group") // NZ) * 2 + lax.axis_index("dev") // (2 * NY)
    ids = expert_ids.reshape(steps, 2 * rows)
    order = jnp.arange(2 * rows)
    earlier = (ids[:, :, None] == ids[:, None, :]) & (order[None, :] < order[:, None])[None]
    slot = jnp.sum(earlier.astype(jnp.int32), 2) + 2 * jnp.arange(steps)[:, None]
    pad = ((0, 0), (0, 8 - rows), (0, 0))
    ids = jnp.pad(ids.reshape(steps, rows, 2), pad, constant_values=-1).reshape(16, 2)
    slot = jnp.pad(slot.reshape(steps, rows, 2), pad).reshape(16, 2)
    weight = jnp.pad(combine, pad).reshape(16, 2)
    place = (ids // 4) * 64 + lax.rem(ids, 4) * 16 + x * 4 + slot
    place = jnp.where(ids < 0, -1, place)
    header = jnp.any(place[:, :, None] == jnp.arange(HDR), 1).astype(jnp.bfloat16)
    col = jnp.arange(64)
    expert, col_slot = lax.rem(col // 16, 2) * 4 + lax.rem(col // 4, 4), lax.rem(col, 4)
    hit = (ids[:, :, None] == expert) & (slot[:, :, None] == col_slot)
    wmat = jnp.sum(jnp.where(hit, weight[:, :, None], 0.0), 1)
    high = lax.reduce_precision(wmat, 8, 7)
    rows_in = jnp.pad(expert_input, pad).reshape(16, D)
    msg = jnp.concatenate(
        [rows_in[:, :PW], header, rows_in[:, PW:], high.astype(jnp.bfloat16), (wmat - high).astype(jnp.bfloat16)], 1
    )
    bf, vm = jnp.bfloat16, pltpu.VMEM
    dma = pltpu.SemaphoreType.DMA
    result = pl.pallas_call(
        kernel,
        out_shape=jax.ShapeDtypeStruct((16, D), bf),
        in_specs=[
            pl.BlockSpec(memory_space=pl.ANY),
            pl.BlockSpec(memory_space=pltpu.VMEM),
            pl.BlockSpec(memory_space=pl.ANY),
            pl.BlockSpec(memory_space=pl.ANY),
            pl.BlockSpec(memory_space=pl.ANY),
        ],
        out_specs=pl.BlockSpec(memory_space=pltpu.VMEM),
        scratch_shapes=[
            vm((64, PW + HDR), bf), vm((HDR, 64), bf), vm((64, PW), bf), vm((NZ * BLK, D), bf),
            vm((D, 2 * FFD), bf), vm((D, 2 * FFD), bf), vm((2 * FFD, D), bf),
            vm((NZ * BLK, 2 * FFD), bf), vm((NZ * BLK, D), jnp.float32),
            vm((2, 4, BLK, PW), bf), vm((2, 4, BLK, PW), bf),
            vm((BLK, PW), bf), vm((64, PW), bf), vm((64, PW), bf), vm((64, PW), bf),
            vm((64, 64), bf), vm((NZ, 64, MW), bf),
            vm((NZ, 64, RW), bf), vm((NZ, 64, RW), bf), vm((NZ, 64, RW), bf), vm((NZ, 64, RW), bf), vm((NZ, 64, RW), bf),
            vm((NZ, 16, RW), jnp.float32), vm((2, 4, 16, RW), bf), vm((2, 4, 16, RW), bf),
            dma((2,)), dma((3,)), dma((3,)), dma((3,)),
            dma((3, NC + 1)), dma((3, NC + 1)), dma((3, NC)), dma((3, NC)), dma((NC,)),
            dma((2, 4, NC)), dma((2, 4, NC)), dma((2, 4, NC)), dma((2, 4, NC)),
            dma((3, NC)), dma((3, NC)), dma((NC,)), dma((3, NC)), dma((3, NC)), dma((NC,)),
            dma((2, 4)), dma((2, 4)), dma((NZ, 3)), dma((NZ, 3)), dma((NZ, 3)), dma((NZ, 3)), dma((NZ,)),
            dma((NZ, 3)), dma((NZ, 3)), dma((NZ,)), dma((NZ, 3)), dma((NZ, 3)), dma((NZ,)), dma((2, 4)), dma((2, 4)),
        ],
        compiler_params=pltpu.CompilerParams(
            collective_id=0, has_side_effects=True, vmem_limit_bytes=63 * 2**20
        ),
    )(msg, wmat, gate_weight[0], up_weight[0], down_weight[0])
    return result.reshape(steps, 8, D)[:, :rows]


def solution(mesh):
    in_specs = (
        P(None, ("group", "dev"), None),
        P(None, ("group", "dev"), None),
        P(None, ("group", "dev"), None),
        P("dev", None, "group"),
        P("dev", None, "group"),
        P("dev", "group", None),
    )
    out_specs = P(None, ("group", "dev"), None)
    return jax.shard_map(local, mesh=mesh, in_specs=in_specs, out_specs=out_specs, check_vma=False)
```

```python
import jax
import jax.numpy as jnp
from jax import lax
from jax.experimental import pallas as pl
from jax.experimental.pallas import tpu as pltpu
from jax.sharding import PartitionSpec as P

MESH = pl.DeviceIdType.MESH
NX, NY, NZ = 4, 4, 8
D, FFD = 4096, 384
BLK = 64
NC = 4
CW = 640
PW = NC * CW
RW = D - PW
HDR = 128
XW = HDR + RW
MW = XW + HDR
POS = {0: 0, 1: 1, 7: 2, 2: 3, 6: 4, 3: 5, 5: 6, 4: 7}
GROUPS = ((0, 3), (3, 2), (5, 2), (7, 1))


def kernel(
    msg, wmat, gate, up, down, out,
    raw, hdr_t, sel, xs, wg, wu, wd, h, p, sp, rp, fin, yb, pb, xb,
    perm, xr, selr, finr, ybr, pbr, xbr, pr, spr, rpr,
    own_sem, w_own, w_send, w_recv, x_send, x_recv, y_send, y_recv, y_own,
    g_send, g_recv, r_send, r_recv, b_send, b_recv, b_own, f_send, f_recv, f_own,
    rz_send, rz_recv, rx_send, rx_recv, ry_send, ry_recv, ry_own,
    rb_send, rb_recv, rb_own, rf_send, rf_recv, rf_own, rr_send, rr_recv,
):
    g, d = lax.axis_index("group"), lax.axis_index("dev")
    z, x_hi = lax.rem(g, NZ), g // NZ
    core, y, x_lo = lax.rem(d, 2), lax.rem(d // 2, NY), d // (2 * NY)
    x = x_hi * 2 + x_lo

    def dev(xx, yy, zz, cc):
        return ((xx // 2) * NZ + zz, (lax.rem(xx, 2) * NY + yy) * 2 + cc)

    def x_at(j):
        return dev(lax.rem(x + j, NX), y, z, core)

    def y_at(j):
        return dev(x, lax.rem(y + j, NY), z, core)

    def z_at(j):
        return dev(x, y, lax.rem(z + j, NZ), core)

    other = dev(x, y, z, 1 - core)

    def remote(src, dst, send, recv, to):
        return pltpu.make_async_remote_copy(
            src_ref=src, dst_ref=dst, send_sem=send, recv_sem=recv, device_id=to, device_id_type=MESH
        )

    def cols(c):
        return pl.ds(c * CW, CW)

    def rows16(i):
        return pl.ds(pl.multiple_of(i * 16, 16), 16)

    sends = []

    def start(copy):
        copy.start()
        sends.append(copy)

    own = pltpu.make_async_copy(msg.at[:, pl.ds(0, PW + HDR)], raw.at[pl.ds(0, 16), :], own_sem.at[0])
    own.start()
    own_r = pltpu.make_async_copy(msg.at[:, pl.ds(PW, MW)], xr.at[0, pl.ds(0, 16), :], own_sem.at[1])
    own_r.start()
    w_copies = [
        pltpu.make_async_copy(gate, wg.at[:, pl.ds(0, FFD)], w_own.at[0]),
        pltpu.make_async_copy(up, wu.at[:, pl.ds(0, FFD)], w_own.at[1]),
        pltpu.make_async_copy(down, wd.at[pl.ds(0, FFD), :], w_own.at[2]),
    ]
    barrier = pltpu.get_barrier_semaphore()
    partners = [x_at(j) for j in (1, 2, 3)] + [y_at(j) for j in (1, 2, 3)] + [z_at(1), z_at(NZ - 1), other]
    for partner in partners:
        pl.semaphore_signal(barrier, inc=1, device_id=partner, device_id_type=MESH)
    pl.semaphore_wait(barrier, len(partners))

    a, b = lax.broadcasted_iota(jnp.int32, (64, 64), 0), lax.broadcasted_iota(jnp.int32, (64, 64), 1)
    moved = (b & 3) | ((b >> 4) << 2) | (((b >> 2) & 3) << 4)
    perm[...] = jnp.where(a == moved, 1.0, 0.0).astype(jnp.bfloat16)

    rz_copies = {}

    def rz_start(way, hop):
        k_from, k_to = ((NZ - hop) % NZ, NZ - hop - 1) if way == 0 else (hop, hop + 1)
        part = pl.ds(0, MW) if hop < 3 else pl.ds(way * (MW // 2), MW // 2)
        rows = pl.ds(0, 16)
        source = msg.at[:, pl.ds(PW, MW)] if hop == 0 else xr.at[k_from, rows, part]
        rz_copies[way, hop] = remote(
            source, xr.at[k_to, rows, part], rz_send.at[way, hop], rz_recv.at[way, hop], z_at(1 if way == 0 else NZ - 1)
        )
        start(rz_copies[way, hop])

    rx_copies, ry_copies = {}, {}

    def rx_start(k):
        for j in (1, 3, 2):
            part = pl.ds(0, XW)
            source = msg.at[:, pl.ds(PW, XW)] if k == 0 else xr.at[k, pl.ds(0, 16), part]
            rx_copies[k, j] = remote(
                source, xr.at[k, pl.ds(j * 16, 16), part], rx_send.at[k, j - 1], rx_recv.at[k, j - 1], x_at(j)
            )
            start(rx_copies[k, j])

    def rz_next(hop):
        if hop == 3:
            for way in (0, 1):
                rz_copies[way, 3].wait_recv()
            rx_start(4)
            return
        for way in (0, 1):
            rz_copies[way, hop].wait_recv()
            rz_start(way, hop + 1)
        for way in (0, 1):
            rx_start(NZ - hop - 1 if way == 0 else hop + 1)

    def r_pick(k):
        if k == 0:
            own_r.wait()
        for j in (1, 2, 3):
            rx_copies[k, j].wait_recv()
        hdr_t[...] = xr[k, :, pl.ds(0, HDR)].astype(jnp.float32).T.astype(jnp.bfloat16)
        selr[k] = jnp.dot(
            hdr_t[pl.ds(pl.multiple_of(x_lo * 64, 64), 64), :], xr[k, :, pl.ds(HDR, RW)],
            preferred_element_type=jnp.float32,
        ).astype(jnp.bfloat16)
        target = xs.at[pl.ds(pl.multiple_of(POS[k] * BLK + y * 16, 16), 16), pl.ds(PW, RW)]
        for j in (1, 3, 2):
            ry_copies[k, j] = remote(
                selr.at[k, rows16(lax.rem(y + j, NY)), :], target, ry_send.at[k, j - 1], ry_recv.at[k, j - 1], y_at(j)
            )
            start(ry_copies[k, j])
        ry_copies[k, 0] = pltpu.make_async_copy(selr.at[k, rows16(y), :], target, ry_own.at[k])
        ry_copies[k, 0].start()

    def r_ready(k):
        for j in (1, 2, 3):
            ry_copies[k, j].wait_recv()
        ry_copies[k, 0].wait()

    for way in (0, 1):
        rz_start(way, 0)

    def x_copy(j, c):
        part = pl.ds(PW, HDR) if c == NC else cols(c)
        return remote(
            msg.at[:, part], raw.at[pl.ds(j * 16, 16), part], x_send.at[j - 1, c], x_recv.at[j - 1, c], x_at(j)
        )

    x_copies = {}
    for c in (NC, 0, 1, 2, 3):
        for j in (1, 3, 2):
            x_copies[j, c] = x_copy(j, c)
            start(x_copies[j, c])
    rx_start(0)
    for copy in w_copies:
        copy.start()
    w_remote = [
        remote(gate, wg.at[:, pl.ds(FFD, FFD)], w_send.at[0], w_recv.at[0], other),
        remote(up, wu.at[:, pl.ds(FFD, FFD)], w_send.at[1], w_recv.at[1], other),
        remote(down, wd.at[pl.ds(FFD, FFD), :], w_send.at[2], w_recv.at[2], other),
    ]
    for copy in w_remote:
        start(copy)

    y_copies = {}

    def pick(c):
        if c == 0:
            own.wait()
            for j in (1, 2, 3):
                x_copies[j, NC].wait_recv()
        for j in (1, 2, 3):
            x_copies[j, c].wait_recv()
        hdr_t[...] = raw[:, pl.ds(PW, HDR)].astype(jnp.float32).T.astype(jnp.bfloat16)
        sel[:, cols(c)] = jnp.dot(
            hdr_t[pl.ds(pl.multiple_of(x_lo * 64, 64), 64), :], raw[:, cols(c)], preferred_element_type=jnp.float32
        ).astype(jnp.bfloat16)
        for j in (1, 3, 2):
            to = lax.rem(y + j, NY)
            y_copies[j, c] = remote(
                sel.at[rows16(to), cols(c)], xs.at[rows16(y), cols(c)],
                y_send.at[j - 1, c], y_recv.at[j - 1, c], y_at(j),
            )
            start(y_copies[j, c])
        y_copies[0, c] = pltpu.make_async_copy(
            sel.at[rows16(y), cols(c)], xs.at[rows16(y), cols(c)], y_own.at[c]
        )
        y_copies[0, c].start()

    def block(k):
        return pl.ds(POS[k] * BLK, BLK)

    def g_copy(way, hop, c):
        k_from, k_to = ((NZ - hop) % NZ, NZ - hop - 1) if way == 0 else (hop, hop + 1)
        return remote(
            xs.at[block(k_from), cols(c)], xs.at[block(k_to), cols(c)],
            g_send.at[way, hop, c], g_recv.at[way, hop, c], z_at(1 if way == 0 else NZ - 1),
        )

    def far(way):
        return (0, 1) if way == 0 else (2, 3)

    g_copies = {}

    def g_start(way, hop, c):
        g_copies[way, hop, c] = g_copy(way, hop, c)
        start(g_copies[way, hop, c])

    order = {0: (0, 1, 2, 3), 1: (2, 3, 0, 1)}

    def z_first(c):
        for j in (1, 2, 3):
            y_copies[j, c].wait_recv()
        y_copies[0, c].wait()
        for way in (0, 1):
            g_start(way, 0, c)

    def z_next(hop, which):
        for i in which:
            for way in (0, 1):
                c = order[way][i]
                if hop == 3 and c not in far(way):
                    continue
                g_copies[way, hop, c].wait_recv()
                if hop < 2 or (hop == 2 and c in far(way)):
                    g_start(way, hop + 1, c)

    pick(0)
    rz_next(0)
    pick(1)
    z_first(0)
    rz_next(1)
    pick(2)
    z_first(1)
    pick(3)
    rz_next(2)
    z_first(2)
    z_first(3)
    rz_next(3)

    def gate_up(group, n):
        first, count = GROUPS[group]
        rows, part = pl.ds(first * BLK, count * BLK), pl.ds(n * 256, 256)
        gate_val = jnp.dot(xs[rows, :], wg[:, part], preferred_element_type=jnp.float32)
        up_val = jnp.dot(xs[rows, :], wu[:, part], preferred_element_type=jnp.float32)
        h[rows, part] = (jax.nn.silu(gate_val) * up_val).astype(jnp.bfloat16)

    def down_proj(group, quarter):
        first, count = GROUPS[group]
        rows = pl.ds(first * BLK, count * BLK)

        def tile(n, carry):
            part = pl.ds(pl.multiple_of(n * 256, 256), 256)
            p[rows, part] = jnp.dot(h[rows, :], wd[:, part], preferred_element_type=jnp.float32)
            return carry

        lax.fori_loop(quarter * 4, quarter * 4 + 4, tile, 0)

    def held(way, hop):
        return 4 - hop if way == 0 else (4 + hop) % NZ

    r_copies = {}

    def r_start(way, hop, c):
        r_copies[way, hop, c] = remote(
            sp.at[way, hop, :, cols(c)], rp.at[way, hop, :, cols(c)],
            r_send.at[way, hop, c], r_recv.at[way, hop, c], z_at(1 if way == 0 else NZ - 1),
        )
        start(r_copies[way, hop, c])

    def r_own(way, hop, c):
        sp[way, hop, :, cols(c)] = p[block(held(way, hop)), cols(c)].astype(jnp.bfloat16)
        r_start(way, hop, c)

    def r_add(way, hop, c):
        r_copies[way, hop - 1, c].wait_recv()
        sp[way, hop, :, cols(c)] = (
            p[block(held(way, hop)), cols(c)] + rp[way, hop - 1, :, cols(c)].astype(jnp.float32)
        ).astype(jnp.bfloat16)
        r_start(way, hop, c)

    near = {0: (2, 3), 1: (0, 1)}

    def r_adds(which, step):
        for i in (0, 1):
            for way in (0, 1):
                r_add(way, step, which[way][i])

    rb_copies, rf_copies, rr_copies = {}, {}, {}

    def r_back_y(k):
        finr[k] = p[block(k), pl.ds(PW, RW)].astype(jnp.bfloat16)
        for j in (1, 3, 2):
            rb_copies[k, j] = remote(
                finr.at[k, rows16(lax.rem(y + j, NY)), :], ybr.at[k, rows16(y), :],
                rb_send.at[k, j - 1], rb_recv.at[k, j - 1], y_at(j),
            )
            start(rb_copies[k, j])
        rb_copies[k, 0] = pltpu.make_async_copy(finr.at[k, rows16(y), :], ybr.at[k, rows16(y), :], rb_own.at[k])
        rb_copies[k, 0].start()

    def r_back_x(k):
        for j in (1, 2, 3):
            rb_copies[k, j].wait_recv()
        rb_copies[k, 0].wait()
        pbr[k] = jnp.dot(perm[...], ybr[k], preferred_element_type=jnp.float32).astype(jnp.bfloat16)
        for j in (1, 3, 2):
            rf_copies[k, j] = remote(
                pbr.at[k, rows16(lax.rem(x + j, NX)), :], xbr.at[k, rows16(x), :],
                rf_send.at[k, j - 1], rf_recv.at[k, j - 1], x_at(j),
            )
            start(rf_copies[k, j])
        rf_copies[k, 0] = pltpu.make_async_copy(pbr.at[k, rows16(x), :], xbr.at[k, rows16(x), :], rf_own.at[k])
        rf_copies[k, 0].start()

    def r_weigh(k):
        for j in (1, 2, 3):
            rf_copies[k, j].wait_recv()
        rf_copies[k, 0].wait()
        weights = xr[k, pl.ds(0, 16), pl.ds(XW, HDR)]
        values = xbr[k]
        pr[k] = jnp.dot(weights, jnp.concatenate([values, values], 0), preferred_element_type=jnp.float32)

    def rr_step(way, hop):
        part = pl.ds(0, RW) if hop else pl.ds(way * (RW // 2), RW // 2)
        k = held(way, hop)
        total = pr[k, :, part]
        if hop:
            rr_copies[way, hop - 1].wait_recv()
            if hop == 1:
                half = pl.ds(way * (RW // 2), RW // 2)
                pr[k, :, half] = pr[k, :, half] + rpr[way, 0, :, half].astype(jnp.float32)
                total = pr[k, :, part]
            else:
                total = total + rpr[way, hop - 1, :, part].astype(jnp.float32)
        spr[way, hop, :, part] = total.astype(jnp.bfloat16)
        rr_copies[way, hop] = remote(
            spr.at[way, hop, :, part], rpr.at[way, hop, :, part],
            rr_send.at[way, hop], rr_recv.at[way, hop], z_at(1 if way == 0 else NZ - 1),
        )
        start(rr_copies[way, hop])

    def rr_steps(hop):
        for way in (0, 1):
            rr_step(way, hop)

    def r_finish():
        for way in (0, 1):
            rr_copies[way, 3].wait_recv()
        out[:, pl.ds(PW, RW)] = (
            pr[0] + rpr[0, 3].astype(jnp.float32) + rpr[1, 3].astype(jnp.float32)
        ).astype(jnp.bfloat16)

    r_pick(0)
    z_next(0, (0,))
    r_pick(7)
    z_next(0, (1, 2))
    r_pick(1)
    z_next(0, (3,))
    for copy in w_copies[:2]:
        copy.wait()
    for copy in w_remote[:2]:
        copy.wait_recv()
    for k in (0, 7, 1):
        r_ready(k)
    gate_up(0, 0)
    r_pick(6)
    z_next(1, (0,))
    gate_up(0, 1)
    z_next(1, (1,))
    r_pick(2)
    gate_up(0, 2)
    w_copies[2].wait()
    w_remote[2].wait_recv()
    z_next(1, (2,))
    down_proj(0, 0)
    down_proj(0, 1)
    z_next(1, (3,))
    r_pick(5)
    down_proj(0, 2)
    down_proj(0, 3)
    r_ready(6)
    r_ready(2)
    gate_up(1, 0)
    z_next(2, (0,))
    r_pick(3)
    gate_up(1, 1)
    z_next(2, (1,))
    r_pick(4)
    gate_up(1, 2)
    z_next(2, (2,))
    for k in (0, 7, 1):
        r_back_y(k)
    down_proj(1, 0)
    down_proj(1, 1)
    z_next(2, (3,))
    down_proj(1, 2)
    down_proj(1, 3)
    r_ready(5)
    r_ready(3)
    r_back_y(6)
    r_back_y(2)
    gate_up(2, 0)
    r_back_x(0)
    gate_up(2, 1)
    r_back_x(7)
    gate_up(2, 2)
    r_back_x(1)
    for quarter in range(4):
        down_proj(2, quarter)
    for i in (0, 1):
        for way in (0, 1):
            r_own(way, 1, near[way][i])
    r_back_y(5)
    r_back_y(3)
    z_next(3, (0, 1))
    r_ready(4)
    gate_up(3, 0)
    r_back_x(6)
    gate_up(3, 1)
    r_back_x(2)
    gate_up(3, 2)
    down_proj(3, 0)
    r_own(0, 0, 0)
    down_proj(3, 1)
    r_own(0, 0, 1)
    down_proj(3, 2)
    r_own(1, 0, 2)
    down_proj(3, 3)
    r_own(1, 0, 3)
    r_back_y(4)
    r_back_x(5)
    r_back_x(3)
    r_adds(near, 2)
    for k in (0, 7, 1):
        r_weigh(k)
    r_adds({0: far(0), 1: far(1)}, 1)
    r_back_x(4)
    for k in (6, 2):
        r_weigh(k)
    r_adds(near, 3)
    for k in (5, 3):
        r_weigh(k)
    r_adds({0: far(0), 1: far(1)}, 2)
    r_weigh(4)
    rr_steps(0)
    r_adds({0: far(0), 1: far(1)}, 3)
    rr_steps(1)
    b_copies = {}

    def back_y(c):
        for way in (0, 1):
            r_copies[way, 3, c].wait_recv()
        fin[:, cols(c)] = (
            p[block(0), cols(c)]
            + rp[0, 3, :, cols(c)].astype(jnp.float32)
            + rp[1, 3, :, cols(c)].astype(jnp.float32)
        ).astype(jnp.bfloat16)
        for j in (1, 3, 2):
            to = lax.rem(y + j, NY)
            b_copies[j, c] = remote(
                fin.at[rows16(to), cols(c)], yb.at[rows16(y), cols(c)],
                b_send.at[j - 1, c], b_recv.at[j - 1, c], y_at(j),
            )
            start(b_copies[j, c])
        b_copies[0, c] = pltpu.make_async_copy(
            fin.at[rows16(y), cols(c)], yb.at[rows16(y), cols(c)], b_own.at[c]
        )
        b_copies[0, c].start()

    f_copies = {}

    def back_x(c):
        for j in (1, 2, 3):
            b_copies[j, c].wait_recv()
        b_copies[0, c].wait()
        pb[:, cols(c)] = jnp.dot(perm[...], yb[:, cols(c)], preferred_element_type=jnp.float32).astype(jnp.bfloat16)
        for j in (1, 3, 2):
            to = lax.rem(x + j, NX)
            f_copies[j, c] = remote(
                pb.at[rows16(to), cols(c)], xb.at[rows16(x), cols(c)],
                f_send.at[j - 1, c], f_recv.at[j - 1, c], x_at(j),
            )
            start(f_copies[j, c])
        f_copies[0, c] = pltpu.make_async_copy(
            pb.at[rows16(x), cols(c)], xb.at[rows16(x), cols(c)], f_own.at[c]
        )
        f_copies[0, c].start()

    def finish(c):
        for j in (1, 2, 3):
            f_copies[j, c].wait_recv()
        f_copies[0, c].wait()
        out[:, cols(c)] = jnp.dot(
            wmat[...], xb[:, cols(c)].astype(jnp.float32),
            preferred_element_type=jnp.float32, precision=lax.Precision.HIGHEST,
        ).astype(jnp.bfloat16)

    back_y(0)
    back_y(2)
    rr_steps(2)
    back_x(0)
    back_y(1)
    back_x(2)
    back_y(3)
    rr_steps(3)
    finish(0)
    back_x(1)
    finish(2)
    back_x(3)
    r_finish()
    finish(1)
    finish(3)
    for copy in sends:
        copy.wait_send()


def local(expert_input, expert_ids, combine, gate_weight, up_weight, down_weight):
    steps, rows = expert_input.shape[0], expert_input.shape[1]
    x = (lax.axis_index("group") // NZ) * 2 + lax.axis_index("dev") // (2 * NY)
    ids = expert_ids.reshape(steps, 2 * rows)
    order = jnp.arange(2 * rows)
    earlier = (ids[:, :, None] == ids[:, None, :]) & (order[None, :] < order[:, None])[None]
    slot = jnp.sum(earlier.astype(jnp.int32), 2) + 2 * jnp.arange(steps)[:, None]
    pad = ((0, 0), (0, 8 - rows), (0, 0))
    ids = jnp.pad(ids.reshape(steps, rows, 2), pad, constant_values=-1).reshape(16, 2)
    slot = jnp.pad(slot.reshape(steps, rows, 2), pad).reshape(16, 2)
    weight = jnp.pad(combine, pad).reshape(16, 2)
    place = (ids // 4) * 64 + lax.rem(ids, 4) * 16 + x * 4 + slot
    place = jnp.where(ids < 0, -1, place)
    header = jnp.any(place[:, :, None] == jnp.arange(HDR), 1).astype(jnp.bfloat16)
    col = jnp.arange(64)
    expert, col_slot = lax.rem(col // 16, 2) * 4 + lax.rem(col // 4, 4), lax.rem(col, 4)
    hit = (ids[:, :, None] == expert) & (slot[:, :, None] == col_slot)
    wmat = jnp.sum(jnp.where(hit, weight[:, :, None], 0.0), 1)
    high = lax.reduce_precision(wmat, 8, 7)
    rows_in = jnp.pad(expert_input, pad).reshape(16, D)
    msg = jnp.concatenate(
        [rows_in[:, :PW], header, rows_in[:, PW:], high.astype(jnp.bfloat16), (wmat - high).astype(jnp.bfloat16)], 1
    )
    bf, vm = jnp.bfloat16, pltpu.VMEM
    dma = pltpu.SemaphoreType.DMA
    result = pl.pallas_call(
        kernel,
        out_shape=jax.ShapeDtypeStruct((16, D), bf),
        in_specs=[
            pl.BlockSpec(memory_space=pl.ANY),
            pl.BlockSpec(memory_space=pltpu.VMEM),
            pl.BlockSpec(memory_space=pl.ANY),
            pl.BlockSpec(memory_space=pl.ANY),
            pl.BlockSpec(memory_space=pl.ANY),
        ],
        out_specs=pl.BlockSpec(memory_space=pltpu.VMEM),
        scratch_shapes=[
            vm((64, PW + HDR), bf), vm((HDR, 64), bf), vm((64, PW), bf), vm((NZ * BLK, D), bf),
            vm((D, 2 * FFD), bf), vm((D, 2 * FFD), bf), vm((2 * FFD, D), bf),
            vm((NZ * BLK, 2 * FFD), bf), vm((NZ * BLK, D), jnp.float32),
            vm((2, 4, BLK, PW), bf), vm((2, 4, BLK, PW), bf),
            vm((BLK, PW), bf), vm((64, PW), bf), vm((64, PW), bf), vm((64, PW), bf),
            vm((64, 64), bf), vm((NZ, 64, MW), bf),
            vm((NZ, 64, RW), bf), vm((NZ, 64, RW), bf), vm((NZ, 64, RW), bf), vm((NZ, 64, RW), bf), vm((NZ, 64, RW), bf),
            vm((NZ, 16, RW), jnp.float32), vm((2, 4, 16, RW), bf), vm((2, 4, 16, RW), bf),
            dma((2,)), dma((3,)), dma((3,)), dma((3,)),
            dma((3, NC + 1)), dma((3, NC + 1)), dma((3, NC)), dma((3, NC)), dma((NC,)),
            dma((2, 4, NC)), dma((2, 4, NC)), dma((2, 4, NC)), dma((2, 4, NC)),
            dma((3, NC)), dma((3, NC)), dma((NC,)), dma((3, NC)), dma((3, NC)), dma((NC,)),
            dma((2, 4)), dma((2, 4)), dma((NZ, 3)), dma((NZ, 3)), dma((NZ, 3)), dma((NZ, 3)), dma((NZ,)),
            dma((NZ, 3)), dma((NZ, 3)), dma((NZ,)), dma((NZ, 3)), dma((NZ, 3)), dma((NZ,)), dma((2, 4)), dma((2, 4)),
        ],
        compiler_params=pltpu.CompilerParams(
            collective_id=0, has_side_effects=True, vmem_limit_bytes=63 * 2**20
        ),
    )(msg, wmat, gate_weight[0], up_weight[0], down_weight[0])
    return result.reshape(steps, 8, D)[:, :rows]


def solution(mesh):
    in_specs = (
        P(None, ("group", "dev"), None),
        P(None, ("group", "dev"), None),
        P(None, ("group", "dev"), None),
        P("dev", None, "group"),
        P("dev", None, "group"),
        P("dev", "group", None),
    )
    out_specs = P(None, ("group", "dev"), None)
    return jax.shard_map(local, mesh=mesh, in_specs=in_specs, out_specs=out_specs, check_vma=False)
```
